32 devices in a mesh: dom: 8 (over z, y), lev: 4 (over x, core).
Axes of the slice: x: 2, y: 2, z: 4, core: 2. Of those that a mesh axis runs over, the one named last changes fastest.
Arguments:
- state: float32 [2, 32, 8192], P(None, 'lev', 'dom'), may hold values from -6 to 6
- neighbours: int32 [7, 8192], P(None, 'dom'), may hold values from -1 to 1279, as said below
- edge_coef: float32 [7, 8192], P(None, 'dom'), may hold values from 0.05 to 0.45
- send_lists: int32 [8, 2, 128], P('dom'), may hold values from 0 to 1023, as said below
- vert_coef: float32 [2], replicated, may hold values from 0.1 to 0.45
- w_lw: bfloat16 [64, 4096], replicated, may hold values from -0.75 to 0.75
- w_sw: bfloat16 [64, 4096], replicated, may hold values from -0.75 to 0.75
- g_weight: float32 [2, 128], replicated, may hold values from 0.25 to 4
- day: int32 [8192], P(('dom', 'lev')), may hold values from 0 to 1, as said below
- cos_zenith: float32 [8192], P(('dom', 'lev')), may hold values from 0.05 to 1
- owner_map: int32 [8192], P(('dom', 'lev')), may hold values from 0 to 511, as said below
Outputs:
- new_state: float32 [2, 32, 8192], P(None, 'lev', 'dom')
- heating: bfloat16 [32, 8192], P(None, ('dom', 'lev'))
- owner_flux: float32 [16384], P(('dom', 'lev'))
The draws below stay inside these ranges and needn't reach their ends.
Inputs may be any that keep to these rules, and one draw needn't show every extreme that they name: `neighbours`: entries are -1 (padding, after 5 to 7 valid entries of a cell) or an index into the partition's extended numbering: own cells, then 128 cells from the west partition, then 128 from the east; every halo position is named by some cell. `send_lists`: each row holds 128 distinct local cell numbers of the sending partition. `day`: the daylit columns form one run of consecutive column numbers, wrapping around at the end, that holds half of all columns. `owner_map`: the 256 columns of one device (aligned blocks along the cells) take distinct slots; at most 64 columns of one device go to one owner, and one owner receives 64 from every device; each owner's share of a device's daylit columns is in proportion to the slots it receives from that device.
All inputs are finite; a program needn't handle non-finite values.
Results may differ from the reference program's by a relative error of at most 0.005.
Values may be sent and summed in bfloat16 or wider, within the bound.
No kernel may reach another device: no remote copies, remote signals or barrier semaphores. Data moves between devices by JAX's collectives and lax.ppermute only.
A program may use at most 64 MiB of HBM per device.

```python
import math
import jax
import jax.numpy as jnp
from jax import lax

CELLS_DEV = 1024
LEVELS = 32
G = 128
NEIGH = 7
HALO = 128
CQ = 256
CAP = 64
CELLS = 8192
N_DOM = 8
N_LEV = 4


def draw_neighbours(key, part):
    local_cell = jnp.arange(CELLS, dtype=jnp.int32) % CELLS_DEV
    key_count, key_offset = jax.random.split(key)
    valid_count = jax.random.randint(key_count, (CELLS,), 5, NEIGH + 1)
    offsets = jax.random.randint(key_offset, (NEIGH, CELLS), 0, CELLS_DEV - 1)
    others = (local_cell[None, :] + 1 + offsets) % CELLS_DEV
    first_link = jnp.where(local_cell < 2 * HALO, CELLS_DEV + local_cell, others[0])
    second_link = jnp.where((local_cell >= 2 * HALO) & (local_cell < 4 * HALO), CELLS_DEV + local_cell - 2 * HALO, others[1])
    links = others.at[0].set(first_link).at[1].set(second_link)
    position = jnp.arange(NEIGH, dtype=jnp.int32)[:, None]
    return jnp.where(position < valid_count[None, :], links, -1).astype(jnp.int32)


def draw_send_lists(key, part):
    key_list = jax.random.split(key, N_DOM * 2)
    chosen = jax.vmap(lambda single: jax.random.permutation(single, CELLS_DEV)[:HALO])(key_list)
    return chosen.reshape(N_DOM, 2, HALO).astype(jnp.int32)


def daylight_band(key):
    start_cell = jax.random.randint(jax.random.fold_in(key, 11), (), 0, CELLS)
    column_ids = jnp.arange(CELLS, dtype=jnp.int32)
    shifted = (column_ids - start_cell + CELLS) % CELLS
    return (shifted < CELLS // 2).astype(jnp.int32)


def draw_day(key, part):
    return daylight_band(key)


def draw_owner_map(key, part):
    slot_total = 2 * CQ
    day_flags = daylight_band(key).reshape(CELLS // CQ, CQ)
    full_owner = jax.random.randint(jax.random.fold_in(key, 7), (), 0, N_DOM)
    slot_ids = jnp.arange(slot_total, dtype=jnp.int32)
    owner_of = slot_ids // CAP
    within = slot_ids % CAP
    other_rank = jnp.where(owner_of < full_owner, owner_of, owner_of - 1)
    order_index = within * (N_DOM - 1) + other_rank
    taken_other = order_index < CQ - CAP
    big_key = CAP * CQ + slot_ids
    slot_key = jnp.where(owner_of == full_owner, within * (CQ - CAP), jnp.where(taken_other, order_index * CAP, big_key))
    slot_order = jnp.argsort(slot_key.astype(jnp.int32))[:CQ].astype(jnp.int32)
    key_list = jax.random.split(jax.random.fold_in(key, 13), CELLS // CQ)

    def one_block(single, flags):
        shuffle = jax.random.permutation(single, CQ).astype(jnp.int32)
        column_key = (1 - flags) * CQ + shuffle
        column_order = jnp.argsort(column_key.astype(jnp.int32)).astype(jnp.int32)
        return jnp.zeros((CQ,), jnp.int32).at[column_order].set(slot_order)
    return jax.vmap(one_block)(key_list, day_flags).reshape(CELLS).astype(jnp.int32)


def steps_of(key, dims, shards, smallest, high):
    factor_of, own = 1.0, jax.random.fold_in(key, 6)
    for axis_at, shards_of in shards:
        heights = jnp.exp(jax.random.uniform(jax.random.fold_in(own, axis_at), (shards_of,), jnp.float32, smallest / len(shards), high / len(shards)))
        factor_of = factor_of * jnp.repeat(heights, dims[axis_at] // shards_of).reshape([-1 if axis == axis_at else 1 for axis in range(len(dims))])
    return factor_of


def centred(key, shape, width, most, shards=(), kind=jnp.bfloat16):
    level = steps_of(key, shape, shards, -0.22, 0.18) if shards else 1.0
    entries = jax.random.normal(key, shape, jnp.float32) * width * level
    return jnp.minimum(jnp.maximum(entries, -most), most).astype(kind)


def setup_inputs(seed: int = 0) -> dict:
    key_of = jax.random.split(jax.random.key(seed), 12)
    return {
        "state": centred(key_of[0], (2, LEVELS, CELLS), 1.0, 6.0, ((1, 4), (2, 8)), jnp.float32),
        "neighbours": draw_neighbours(jax.random.fold_in(key_of[11], 71), 0),
        "edge_coef": jnp.clip(0.05 + 0.39999999 * jax.random.uniform(key_of[2], (NEIGH, CELLS), jnp.float32) ** steps_of(key_of[2], (NEIGH, CELLS), ((1, 8),), -0.2, 0.2), 0.05, 0.45),
        "send_lists": draw_send_lists(jax.random.fold_in(key_of[11], 71), 0),
        "vert_coef": jnp.clip(jax.random.uniform(key_of[4], (2,), jnp.float32, 0.1, 0.45), 0.1, 0.45),
        "w_lw": centred(key_of[5], (2 * LEVELS, LEVELS * G), (2 * LEVELS) ** -0.5, 0.75),
        "w_sw": centred(key_of[6], (2 * LEVELS, LEVELS * G), (2 * LEVELS) ** -0.5, 0.75),
        "g_weight": jnp.clip(jnp.exp(jax.random.uniform(key_of[7], (2, G), jnp.float32, math.log(0.25), math.log(4.0))), 0.25, 4.0),
        "day": draw_day(jax.random.fold_in(key_of[11], 71), 0),
        "cos_zenith": jnp.clip(0.05 + 0.95 * jax.random.uniform(key_of[9], (CELLS,), jnp.float32) ** steps_of(key_of[9], (CELLS,), ((0, 32),), -0.2, 0.2), 0.05, 1.0),
        "owner_map": draw_owner_map(jax.random.fold_in(key_of[11], 71), 0),
    }


def tendency(fields, neighbours, edge_coef, send_lists, vert_coef):
    blocked = fields.reshape(2, LEVELS, N_DOM, CELLS_DEV)
    halo_shape = (2, LEVELS, N_DOM, HALO)
    to_west = jnp.take_along_axis(blocked, jnp.broadcast_to(send_lists[None, None, :, 0, :].astype(jnp.int32), halo_shape), axis=3)
    to_east = jnp.take_along_axis(blocked, jnp.broadcast_to(send_lists[None, None, :, 1, :].astype(jnp.int32), halo_shape), axis=3)
    from_west = jnp.roll(to_east, 1, axis=2)
    from_east = jnp.roll(to_west, -1, axis=2)
    extended = jnp.concatenate([blocked, from_west, from_east], axis=3)
    links = neighbours.reshape(NEIGH, N_DOM, CELLS_DEV)
    weights = jnp.where(links >= 0, edge_coef.reshape(NEIGH, N_DOM, CELLS_DEV), 0.0)
    safe_links = jnp.where(links >= 0, links, 0).astype(jnp.int32)
    total = jnp.zeros_like(blocked)
    for neighbour in range(NEIGH):
        chosen = jnp.broadcast_to(safe_links[neighbour][None, None], (2, LEVELS, N_DOM, CELLS_DEV))
        picked = jnp.take_along_axis(extended, chosen, axis=3)
        total = total + weights[neighbour] * (picked - blocked)
    zero_layer = jnp.zeros((2, 1, N_DOM, CELLS_DEV), blocked.dtype)
    above = jnp.concatenate([blocked[:, 1:], zero_layer], axis=1)
    below = jnp.concatenate([zero_layer, blocked[:, :-1]], axis=1)
    total = total + vert_coef[:, None, None, None] * (above - 2.0 * blocked + below)
    return total.reshape(2, LEVELS, CELLS)


def radiate(features, sun, w_lw, w_sw, g_weight):
    heats = []
    bottoms = []
    for band_index, weight in enumerate((w_lw, w_sw)):
        optical = lax.dot_general(weight, features, (((0,), (0,)), ((), ())), preferred_element_type=jnp.float32)
        optical = jax.nn.softplus(optical).reshape(LEVELS, G, -1) * (1.5 / LEVELS)
        summed = jnp.cumsum(optical, axis=0)
        absorbed = jnp.exp(optical - summed) - jnp.exp(-summed)
        heats.append((LEVELS / G) * jnp.einsum("g,lgn->ln", g_weight[band_index], absorbed))
        bottoms.append(jnp.einsum("g,gn->n", g_weight[band_index], jnp.exp(-summed[-1])) / G)
    return sun[None, :] * heats[1] - heats[0], bottoms[0] + sun * bottoms[1]


def reference(state, neighbours, edge_coef, send_lists, vert_coef, w_lw, w_sw, g_weight, day, cos_zenith, owner_map):
    middle = state + tendency(state, neighbours, edge_coef, send_lists, vert_coef) / 3.0
    new_state = state + tendency(middle, neighbours, edge_coef, send_lists, vert_coef) * 0.5
    columns = new_state.astype(jnp.bfloat16).reshape(2 * LEVELS, CELLS)
    sun = (day.astype(jnp.float32) * cos_zenith).astype(jnp.bfloat16).astype(jnp.float32)
    blocks = CELLS // CQ
    feature_blocks = columns.reshape(2 * LEVELS, blocks, CQ).transpose(1, 0, 2)
    sun_blocks = sun.reshape(blocks, CQ)

    def one_block(pair):
        return radiate(pair[0], pair[1], w_lw, w_sw, g_weight)

    heat_blocks, bottom_blocks = lax.map(one_block, (feature_blocks, sun_blocks))
    heating = heat_blocks.transpose(1, 0, 2).reshape(LEVELS, CELLS).astype(jnp.bfloat16)
    surface = bottom_blocks.reshape(CELLS)
    column_ids = jnp.arange(CELLS, dtype=jnp.int32)
    block_ids = column_ids // CQ
    part_ids = block_ids // N_LEV
    level_ids = block_ids % N_LEV
    owners = owner_map // CAP
    within = owner_map % CAP
    position = ((owners * N_LEV + level_ids) * (2 * CQ) + part_ids * CAP + within).astype(jnp.int32)
    owner_flux = jnp.zeros((2 * CELLS,), jnp.float32).at[position].set(surface)
    return new_state, heating, owner_flux
```

```python
import functools
import math

import jax
import jax.numpy as jnp
from jax import lax
from jax.experimental import pallas as pl
from jax.experimental.pallas import tpu as pltpu
from jax.sharding import PartitionSpec as P

NEIGH = 7
LOG2E = 1.0 / math.log(2.0)


def padded(block, sides, width, periodic):
    for axis, dim in sides:
        count = lax.axis_size(axis)
        forward = [(i, i + 1) for i in range(count - 1)]
        if periodic:
            forward.append((count - 1, 0))
        backward = [(target, source) for source, target in forward]
        low = lax.ppermute(
            lax.slice_in_dim(block, block.shape[dim] - width, None, axis=dim), axis, forward
        )
        high = lax.ppermute(lax.slice_in_dim(block, 0, width, axis=dim), axis, backward)
        block = jnp.concatenate([low, block, high], axis=dim)
    return block


def tendency(fields, neighbours, edge_coef, send_lists, vert_coef):
    halo_cells = send_lists.shape[2]
    outgoing = jnp.concatenate(
        [jnp.take(fields, send_lists[0, 0], axis=2), jnp.take(fields, send_lists[0, 1], axis=2)],
        axis=2,
    )
    bordered = padded(outgoing, (("dom", 2),), halo_cells, True)
    extended = jnp.concatenate(
        [fields, bordered[:, :, :halo_cells], bordered[:, :, 3 * halo_cells :]], axis=2
    )
    valid = neighbours >= 0
    weights = jnp.where(valid, edge_coef, 0.0)
    safe_links = jnp.where(valid, neighbours, 0)
    total = jnp.zeros_like(fields)
    for neighbour in range(NEIGH):
        picked = jnp.take(extended, safe_links[neighbour], axis=2)
        total = total + weights[neighbour] * (picked - fields)
    stacked = padded(fields, (("lev", 1),), 1, False)
    total = total + vert_coef[:, None, None] * (stacked[:, 2:] - 2.0 * fields + stacked[:, :-2])
    return total


def radiate_kernel(
    levels, feat_ref, sun_ref, owner_ref, wlw_ref, wsw_ref, gw_ref, heat_ref, flux_ref, acc, gwb, tot
):
    cols = feat_ref.shape[1]
    spectral = gw_ref.shape[1]
    owners, cap = flux_ref.shape
    groups = spectral // 8
    chunk = 16
    scale = -1.5 / levels * LOG2E
    for b in range(2):
        wide = jnp.broadcast_to(gw_ref[b : b + 1, :], (spectral, spectral))
        gwb[b] = jnp.transpose(wide)
        tot[b, 0] = jnp.broadcast_to(
            jnp.sum(gwb[b].reshape(groups, 8, spectral), axis=0)[:, :1], (8, cols)
        )
        acc[b] = jnp.zeros((spectral, cols), jnp.float32)

    def level(l, carry):
        for b, w_ref in enumerate((wlw_ref, wsw_ref)):
            w = w_ref[:, pl.ds(pl.multiple_of(l * spectral, spectral), spectral)]
            x = lax.dot_general(
                w, feat_ref[...], (((0,), (0,)), ((), ())), preferred_element_type=jnp.float32
            )
            part = jnp.zeros((8, cols), jnp.float32)
            for r in range(0, spectral, chunk):
                xs = x[r : r + chunk]
                e = jnp.exp2(jnp.abs(xs) * -LOG2E)
                total = acc[b, r : r + chunk] + (jnp.maximum(xs, 0.0) + jnp.log(1.0 + e))
                acc[b, r : r + chunk] = total
                passed = jnp.exp2(total * scale)
                weight = jnp.concatenate([gwb[b, r : r + chunk]] * (cols // spectral), axis=1)
                passed = passed * weight
                for i in range(0, chunk, 8):
                    part = part + passed[i : i + 8]
            tot[b, l + 1] = part
        return carry

    lax.fori_loop(0, levels, level, 0)
    sun = sun_ref[...]
    fraction = levels / spectral
    heats = []
    for b in range(2):
        heats.append(fraction * jnp.sum(tot[b, :levels] - tot[b, 1:], axis=1))
    heat_ref[...] = (sun * heats[1] - heats[0]).astype(jnp.bfloat16)
    bottoms = [jnp.sum(tot[b, levels], axis=0, keepdims=True) / spectral for b in range(2)]
    surface = bottoms[0] + sun * bottoms[1]
    scatter(surface, owner_ref[...], flux_ref, owners, cap, cols)


def scatter(surface, slot, flux_ref, owners, cap, cols):
    high = surface.astype(jnp.bfloat16).astype(jnp.float32)
    rest = surface - high
    mid = rest.astype(jnp.bfloat16).astype(jnp.float32)
    low = rest - mid
    owner = slot // cap
    within = slot - owner * cap
    mine = lax.broadcasted_iota(jnp.int32, (owners, cols), 0) == owner
    terms = jnp.concatenate([jnp.where(mine, term, 0.0) for term in (high, mid, low)], axis=0)
    place = lax.broadcasted_iota(jnp.int32, (cap, cols), 0) == within
    place = jnp.where(place, 1.0, 0.0).astype(jnp.bfloat16)
    out = lax.dot_general(
        terms.astype(jnp.bfloat16),
        place,
        (((1,), (1,)), ((), ())),
        preferred_element_type=jnp.float32,
    )
    flux_ref[...] = (out[:owners] + out[owners : 2 * owners]) + out[2 * owners :]


def radiate(features, sun, owner_map, w_lw, w_sw, g_weight, owners):
    cols = features.shape[1]
    spectral = g_weight.shape[1]
    levels = w_lw.shape[1] // spectral
    cap = 2 * cols // owners
    vmem = pl.BlockSpec(memory_space=pltpu.VMEM)
    return pl.pallas_call(
        functools.partial(radiate_kernel, levels),
        in_specs=[vmem] * 6,
        out_specs=[vmem] * 2,
        out_shape=[
            jax.ShapeDtypeStruct((levels, cols), jnp.bfloat16),
            jax.ShapeDtypeStruct((owners, cap), jnp.float32),
        ],
        scratch_shapes=[
            pltpu.VMEM((2, spectral, cols), jnp.float32),
            pltpu.VMEM((2, spectral, spectral), jnp.float32),
            pltpu.VMEM((2, levels + 1, 8, cols), jnp.float32),
        ],
        name="radiate",
    )(features, sun, owner_map, w_lw, w_sw, g_weight)


def on_device(
    state,
    neighbours,
    edge_coef,
    send_lists,
    vert_coef,
    w_lw,
    w_sw,
    g_weight,
    day,
    cos_zenith,
    owner_map,
):
    middle = state + tendency(state, neighbours, edge_coef, send_lists, vert_coef) / 3.0
    new_state = state + tendency(middle, neighbours, edge_coef, send_lists, vert_coef) * 0.5
    columns = lax.all_to_all(
        new_state.astype(jnp.bfloat16), "lev", split_axis=2, concat_axis=1, tiled=True
    )
    cols = columns.shape[2]
    sun = (day.astype(jnp.float32) * cos_zenith).astype(jnp.bfloat16).astype(jnp.float32)
    heating, flux = radiate(
        columns.reshape(-1, cols),
        sun.reshape(1, cols),
        owner_map.reshape(1, cols),
        w_lw,
        w_sw,
        g_weight,
        lax.axis_size("dom"),
    )
    owner_flux = lax.all_to_all(flux, "dom", split_axis=0, concat_axis=0, tiled=True)
    return (new_state, heating, owner_flux.reshape(-1))


def solution(mesh):
    placed = (
        P(None, "lev", "dom"),
        P(None, "dom"),
        P(None, "dom"),
        P("dom", None, None),
        P(),
        P(),
        P(),
        P(),
        P(("dom", "lev")),
        P(("dom", "lev")),
        P(("dom", "lev")),
    )
    return jax.shard_map(
        on_device,
        mesh=mesh,
        in_specs=placed,
        out_specs=(P(None, "lev", "dom"), P(None, ("dom", "lev")), P(("dom", "lev"))),
        check_vma=False,
    )
```

```python
import functools
import math

import jax
import jax.numpy as jnp
from jax import lax
from jax.experimental import pallas as pl
from jax.experimental.pallas import tpu as pltpu
from jax.sharding import PartitionSpec as P

NEIGH = 7
LOG2E = 1.0 / math.log(2.0)


LANES = 128


def pick(tables, ids):
    within = ids & (LANES - 1)
    block = ids >> 7
    out = None
    for number, rows in tables.items():
        here = block == number
        found = [jnp.take_along_axis(r, within, axis=1, mode="promise_in_bounds") for r in rows]
        if out is None:
            out = [jnp.where(here, f, jnp.zeros_like(f)) for f in found]
        else:
            out = [jnp.where(here, f, o) for f, o in zip(found, out)]
    return out


def spread(row):
    return jnp.broadcast_to(row, (8, LANES))


def blocks_of(ref, count):
    return {
        t: [ref[v, :, t * LANES : (t + 1) * LANES] for v in range(2)] for t in range(count)
    }


def send_kernel(state_ref, nb_ref, coef_ref, lists_ref, near_a, near_b, far_a, far_b, own_ref, nb8, coef8):
    blocks = state_ref.shape[2] // LANES
    nb8[0:NEIGH] = nb_ref[...]
    nb8[NEIGH:8] = jnp.full((1, nb8.shape[1]), -1, jnp.int32)
    coef8[0:NEIGH] = coef_ref[...]
    coef8[NEIGH:8] = jnp.zeros((1, nb8.shape[1]), jnp.float32)
    tables = blocks_of(state_ref, blocks)
    packs = []
    for side in range(2):
        cells = spread(lists_ref[0, side : side + 1, :])
        out = pick(tables, cells)
        span = [slice(t * LANES, (t + 1) * LANES) for t in range(blocks)]
        near = pick({t: [nb8[:, span[t]]] for t in range(blocks)}, cells)[0]
        coef = pick({t: [coef8[:, span[t]]] for t in range(blocks)}, cells)[0]
        coef = jnp.where(near >= 0, coef, 0.0)
        total = jnp.sum(coef, axis=0, keepdims=True)
        part = [-total * o for o in out]
        for k in range(NEIGH):
            found = pick(tables, spread(near[k : k + 1]))
            part = [p + coef[k : k + 1] * f for p, f in zip(part, found)]
        packs.append((out, part, near.astype(jnp.float32), coef))
        for v in range(2):
            own_ref[side, v] = out[v]
    me = lax.axis_index("dom")
    even = me % 2 == 0
    early = me % 4 < 2
    west, east = packs
    for v in range(2):
        near_a[8 * v : 8 * v + 8] = jnp.where(even, east[0][v], west[0][v])
        near_b[8 * v : 8 * v + 8] = jnp.where(even, west[0][v], east[0][v])
        near_a[16 + 8 * v : 24 + 8 * v] = jnp.where(even, east[1][v], west[1][v])
        near_b[16 + 8 * v : 24 + 8 * v] = jnp.where(even, west[1][v], east[1][v])
        far_a[8 * v : 8 * v + 8] = jnp.where(early, east[0][v], west[0][v])
        far_b[8 * v : 8 * v + 8] = jnp.where(early, west[0][v], east[0][v])
    for i in range(2):
        near_a[32 + 8 * i : 40 + 8 * i] = jnp.where(even, east[2 + i], west[2 + i])
        near_b[32 + 8 * i : 40 + 8 * i] = jnp.where(even, west[2 + i], east[2 + i])


def spread_out(tables, nb_ref, coef_ref, at, start):
    for k in range(NEIGH):
        ids = nb_ref[k : k + 1, at]
        coef = jnp.where(ids >= 0, coef_ref[k : k + 1, at], 0.0)
        found = pick(tables, spread(ids))
        start = [s + coef * f for s, f in zip(start, found)]
    return start


def coef_total(nb_ref, coef_ref, at):
    return jnp.sum(jnp.where(nb_ref[:, at] >= 0, coef_ref[:, at], 0.0), axis=0, keepdims=True)


def inner_kernel(state_ref, nb_ref, coef_ref, y_ref):
    blocks = state_ref.shape[2] // LANES
    tables = blocks_of(state_ref, blocks)
    for t in range(blocks):
        at = slice(t * LANES, (t + 1) * LANES)
        total = coef_total(nb_ref, coef_ref, at)
        found = spread_out(tables, nb_ref, coef_ref, at, [-total * r for r in tables[t]])
        for v in range(2):
            y_ref[v, :, at] = found[v]


def vertical(f):
    rows = f.shape[0]
    zero = jnp.zeros_like(f[:1])
    up = jnp.concatenate([f[1:], zero], axis=0)
    down = jnp.concatenate([zero, f[: rows - 1]], axis=0)
    return up - 2.0 * f + down


def step_kernel(
    vert_ref, state_ref, nb_ref, coef_ref, y_ref, own_ref, near_a, near_b, far_a, far_b,
    part_ref, edge_ref, to1, to2, to3, t_own,
):
    cells = state_ref.shape[2]
    blocks = cells // LANES
    me = lax.axis_index("dom")
    even = me % 2 == 0
    early = me % 4 < 2
    west = jnp.where(even, near_b[...], near_a[...])
    east = jnp.where(even, near_a[...], near_b[...])
    far_west = jnp.where(early, far_b[...], far_a[...])
    far_east = jnp.where(early, far_a[...], far_b[...])
    halves = lambda a, start: [a[start : start + 8], a[start + 8 : start + 16]]
    own = [[own_ref[side, v] for v in range(2)] for side in range(2)]

    def rim(pack, tables):
        total = halves(pack, 16)
        ids = pack[32:40].astype(jnp.int32)
        for k in range(NEIGH):
            found = pick(tables, spread(ids[k : k + 1]))
            total = [s + pack[40 + k : 41 + k] * f for s, f in zip(total, found)]
        return [0.5 * s + y * (1.0 / 6.0) for s, y in zip(halves(pack, 0), total)]

    t_tables = {
        blocks: rim(west, {blocks: halves(far_west, 0), blocks + 1: own[0]}),
        blocks + 1: rim(east, {blocks: own[1], blocks + 1: halves(far_east, 0)}),
    }
    rim_tables = {blocks: halves(west, 0), blocks + 1: halves(east, 0)}
    for t in range(blocks):
        at = slice(t * LANES, (t + 1) * LANES)
        y = spread_out(rim_tables, nb_ref, coef_ref, at, [y_ref[v, :, at] for v in range(2)])
        for v in range(2):
            s = state_ref[v, :, at]
            t_own[v, :, at] = 0.5 * s + y[v] * (1.0 / 6.0)
            part_ref[v, :, at] = 0.5 * s + y[v] * (1.0 / 3.0)
    tables = blocks_of(t_own, blocks)
    tables.update(t_tables)
    for t in range(blocks):
        at = slice(t * LANES, (t + 1) * LANES)
        total = coef_total(nb_ref, coef_ref, at)
        z = spread_out(tables, nb_ref, coef_ref, at, [-total * r for r in tables[t]])
        edges = []
        for v in range(2):
            s = state_ref[v, :, at]
            h = part_ref[v, :, at] + (vert_ref[v] * (1.0 / 6.0)) * vertical(s)
            part_ref[v, :, at] = (s + z[v]) + vert_ref[v] * vertical(h)
            edges.append((h[0:1], s[0:1], h[7:8], s[7:8]))
        edge_ref[:, at] = jnp.concatenate([edges[v][i] for i in range(4) for v in range(2)], axis=0)
    lev = lax.axis_index("lev")
    width = to1.shape[1]
    pieces = cells // width
    everything = [edge_ref[:, i * width : (i + 1) * width] for i in range(pieces)]
    for shift, ref in enumerate((to1, to2, to3), start=1):
        at = pl.ds(pl.multiple_of((lev + shift) % pieces * width, width), width)
        rows = [part_ref[0, :, at], part_ref[1, :, at]]
        rows += [edge_ref[:, at]] if shift == 2 else everything
        ref[...] = jnp.concatenate(rows, axis=0).astype(jnp.bfloat16)


def finish_kernel(
    vert_ref, part_ref, edge_ref, from1, from2, from3, day_ref, cos_ref, owner_ref, wlw_ref, wsw_ref, gw_ref,
    new_ref, heat_ref, flux_ref, whole, edges, feat, acc, gwb, tot,
):
    lev = lax.axis_index("lev")
    count = edges.shape[0]
    width = from1.shape[1]
    cells = part_ref.shape[2]
    mine = pl.ds(pl.multiple_of(lev * width, width), width)
    for v in range(2):
        whole[v, pl.ds(pl.multiple_of(lev * 8, 8), 8), :] = part_ref[v, :, mine]
    edges[lev] = edge_ref[:, mine]
    for shift, ref in enumerate((from1, from2, from3), start=1):
        source = (lev + count - shift) % count
        got = ref[...].astype(jnp.float32)
        for v in range(2):
            whole[v, pl.ds(pl.multiple_of(source * 8, 8), 8), :] = got[8 * v : 8 * v + 8]
        if shift == 2:
            edges[source] = got[16:24]
        else:
            for i in range(count):

                @pl.when(lev == i)
                def _():
                    edges[source] = got[16 + 8 * i : 24 + 8 * i]

    for v in range(2):
        c = vert_ref[v]
        a = c * (1.0 / 6.0)
        for b in range(1, count):
            h_low, s_low = edges[b - 1, 4 + v : 5 + v, :], edges[b - 1, 6 + v : 7 + v, :]
            h_high, s_high = edges[b, v : v + 1, :], edges[b, 2 + v : 3 + v, :]
            r = 8 * b
            whole[v, r : r + 1, :] += c * (h_low - 2.0 * a * s_low + a * s_high)
            whole[v, r + 1 : r + 2, :] += (c * a) * s_low
            whole[v, r - 1 : r, :] += c * (h_high - 2.0 * a * s_high + a * s_low)
            whole[v, r - 2 : r - 1, :] += (c * a) * s_high
        feat[v * 8 * count : (v + 1) * 8 * count] = whole[v].astype(jnp.bfloat16)

    below = from1[16:, :].astype(jnp.float32)
    above = from3[16:, :].astype(jnp.float32)
    below = jnp.where(lev > 0, below, 0.0)
    above = jnp.where(lev < count - 1, above, 0.0)
    below = jnp.concatenate([below[8 * i : 8 * i + 8] for i in range(count)], axis=1)
    above = jnp.concatenate([above[8 * i : 8 * i + 8] for i in range(count)], axis=1)
    has_below = jnp.where(lev > 0, 1.0, 0.0)
    has_above = jnp.where(lev < count - 1, 1.0, 0.0)
    for v in range(2):
        c = vert_ref[v]
        a = c * (1.0 / 6.0)
        h_low, s_low = below[4 + v : 5 + v], below[6 + v : 7 + v]
        h_high, s_high = above[v : v + 1], above[2 + v : 3 + v]
        s_first, s_last = edge_ref[2 + v : 3 + v, :], edge_ref[6 + v : 7 + v, :]
        new_ref[v] = part_ref[v]
        new_ref[v, 0:1, :] += c * (h_low - 2.0 * a * s_low + (has_below * a) * s_first)
        new_ref[v, 1:2, :] += (c * a) * s_low
        new_ref[v, 7:8, :] += c * (h_high - 2.0 * a * s_high + (has_above * a) * s_last)
        new_ref[v, 6:7, :] += (c * a) * s_high

    sun = (day_ref[...].astype(jnp.float32) * cos_ref[...]).astype(jnp.bfloat16).astype(jnp.float32)
    radiate_body(
        8 * count, feat, sun, owner_ref, wlw_ref, wsw_ref, gw_ref, heat_ref, flux_ref, acc, gwb, tot
    )


def radiate_body(
    levels, feat_ref, sun, owner_ref, wlw_ref, wsw_ref, gw_ref, heat_ref, flux_ref, acc, gwb, tot
):
    cols = feat_ref.shape[1]
    spectral = gw_ref.shape[1]
    owners, cap = flux_ref.shape
    groups = spectral // 8
    chunk = 16
    scale = -1.5 / levels * LOG2E
    for b in range(2):
        wide = jnp.broadcast_to(gw_ref[b : b + 1, :], (spectral, spectral))
        gwb[b] = jnp.transpose(wide)
        tot[b, 0] = jnp.broadcast_to(
            jnp.sum(gwb[b].reshape(groups, 8, spectral), axis=0)[:, :1], (8, cols)
        )
        acc[b] = jnp.zeros((spectral, cols), jnp.float32)

    def level(l, carry):
        for b, w_ref in enumerate((wlw_ref, wsw_ref)):
            w = w_ref[:, pl.ds(pl.multiple_of(l * spectral, spectral), spectral)]
            x = lax.dot_general(
                w, feat_ref[...], (((0,), (0,)), ((), ())), preferred_element_type=jnp.float32
            )
            part = jnp.zeros((8, cols), jnp.float32)
            for r in range(0, spectral, chunk):
                xs = x[r : r + chunk]
                e = jnp.exp2(jnp.abs(xs) * -LOG2E)
                total = acc[b, r : r + chunk] + (jnp.maximum(xs, 0.0) + jnp.log(1.0 + e))
                acc[b, r : r + chunk] = total
                passed = jnp.exp2(total * scale)
                weight = jnp.concatenate([gwb[b, r : r + chunk]] * (cols // spectral), axis=1)
                passed = passed * weight
                for i in range(0, chunk, 8):
                    part = part + passed[i : i + 8]
            tot[b, l + 1] = part
        return carry

    lax.fori_loop(0, levels, level, 0)
    fraction = levels / spectral
    heats = []
    for b in range(2):
        heats.append(fraction * jnp.sum(tot[b, :levels] - tot[b, 1:], axis=1))
    heat_ref[...] = (sun * heats[1] - heats[0]).astype(jnp.bfloat16)
    bottoms = [jnp.sum(tot[b, levels], axis=0, keepdims=True) / spectral for b in range(2)]
    surface = bottoms[0] + sun * bottoms[1]
    scatter(surface, owner_ref[...], flux_ref, owners, cap, cols)


def scatter(surface, slot, flux_ref, owners, cap, cols):
    high = surface.astype(jnp.bfloat16).astype(jnp.float32)
    rest = surface - high
    mid = rest.astype(jnp.bfloat16).astype(jnp.float32)
    low = rest - mid
    owner = slot // cap
    within = slot - owner * cap
    mine = lax.broadcasted_iota(jnp.int32, (owners, cols), 0) == owner
    terms = jnp.concatenate([jnp.where(mine, term, 0.0) for term in (high, mid, low)], axis=0)
    place = lax.broadcasted_iota(jnp.int32, (cap, cols), 0) == within
    place = jnp.where(place, 1.0, 0.0).astype(jnp.bfloat16)
    out = lax.dot_general(
        terms.astype(jnp.bfloat16),
        place,
        (((1,), (1,)), ((), ())),
        preferred_element_type=jnp.float32,
    )
    flux_ref[...] = (out[:owners] + out[owners : 2 * owners]) + out[2 * owners :]


def call(kernel, outs, scratch, *args, name, scalars=0, cost=None):
    vmem = pl.BlockSpec(memory_space=pltpu.VMEM)
    smem = pl.BlockSpec(memory_space=pltpu.SMEM)
    return pl.pallas_call(
        kernel,
        in_specs=[smem] * scalars + [vmem] * (len(args) - scalars),
        out_specs=[vmem] * len(outs),
        out_shape=[jax.ShapeDtypeStruct(*out) for out in outs],
        scratch_shapes=[pltpu.VMEM(*s) for s in scratch],
        cost_estimate=cost,
        name=name,
    )(*args)


def swap(count, distance, flip):
    pairs = []
    for i in range(count):
        up = (i % (2 * distance) < distance) != flip
        pairs.append((i, (i + distance if up else i - distance) % count))
    return pairs


def on_device(
    state,
    neighbours,
    edge_coef,
    send_lists,
    vert_coef,
    w_lw,
    w_sw,
    g_weight,
    day,
    cos_zenith,
    owner_map,
):
    f32, bf16 = jnp.float32, jnp.bfloat16
    dom, lev = lax.axis_size("dom"), lax.axis_size("lev")
    cells = state.shape[2]
    levels = state.shape[1] * lev
    cols = cells // lev
    spectral = g_weight.shape[1]
    near_a, near_b, far_a, far_b, own = call(
        send_kernel,
        [((48, LANES), f32)] * 2 + [((16, LANES), f32)] * 2 + [((2, 2, 8, LANES), f32)],
        [((8, cells), jnp.int32), ((8, cells), f32)],
        state, neighbours, edge_coef, send_lists,
        name="send",
    )
    near_a = lax.ppermute(near_a, "dom", swap(dom, 1, False))
    near_b = lax.ppermute(near_b, "dom", swap(dom, 1, True))
    far_a = lax.ppermute(far_a, "dom", swap(dom, 2, False))
    far_b = lax.ppermute(far_b, "dom", swap(dom, 2, True))
    (inner,) = call(
        inner_kernel, [(state.shape, f32)], [], state, neighbours, edge_coef,
        name="inner",
        cost=pl.CostEstimate(flops=2000000, bytes_accessed=200000, transcendentals=0),
    )
    part, edge, to1, to2, to3 = call(
        step_kernel,
        [(state.shape, f32), ((8, cells), f32), ((16 + 8 * lev, cols), bf16), ((24, cols), bf16), ((16 + 8 * lev, cols), bf16)],
        [(state.shape, f32)],
        vert_coef, state, neighbours, edge_coef, inner, own, near_a, near_b, far_a, far_b,
        name="step", scalars=1,
    )
    turn = lambda x, shift: lax.ppermute(x, "lev", [(i, (i + shift) % lev) for i in range(lev)])
    new_state, heating, flux = call(
        finish_kernel,
        [(state.shape, f32), ((levels, cols), bf16), ((dom, 2 * cols // dom), f32)],
        [
            ((2, levels, cols), f32), ((lev, 8, cols), f32), ((2 * levels, cols), bf16),
            ((2, spectral, cols), f32), ((2, spectral, spectral), f32), ((2, levels + 1, 8, cols), f32),
        ],
        vert_coef, part, edge, turn(to1, 1), turn(to2, 2), turn(to3, 3),
        day.reshape(1, cols), cos_zenith.reshape(1, cols), owner_map.reshape(1, cols),
        w_lw, w_sw, g_weight,
        name="finish", scalars=1,
    )
    owner_flux = lax.all_to_all(flux, "dom", split_axis=0, concat_axis=0, tiled=True)
    return (new_state, heating, owner_flux.reshape(-1))


def solution(mesh):
    placed = (
        P(None, "lev", "dom"),
        P(None, "dom"),
        P(None, "dom"),
        P("dom", None, None),
        P(),
        P(),
        P(),
        P(),
        P(("dom", "lev")),
        P(("dom", "lev")),
        P(("dom", "lev")),
    )
    return jax.shard_map(
        on_device,
        mesh=mesh,
        in_specs=placed,
        out_specs=(P(None, "lev", "dom"), P(None, ("dom", "lev")), P(("dom", "lev"))),
        check_vma=False,
    )
```
